32 devices in a mesh: tile: 8 (over z, core), grp: 4 (over y, x).
Axes of the slice: x: 2, y: 2, z: 4, core: 2. Of those that a mesh axis runs over, the one named last changes fastest.
Arguments:
- spectra: bfloat16 [128, 16, 1024], P(('tile', 'grp')), may hold values from -320 to 320
- validity: int32 [128, 16], P(('tile', 'grp')), may hold values 0 or 1
- source_lists: int32 [8, 4, 16], P(None, 'grp'), may hold values from 0 to 127, as said below
Outputs:
- correlations: bfloat16 [8, 4, 16, 16, 2048], P('tile', 'grp')
The draws below stay inside these ranges and needn't reach their ends.
Inputs may be any that keep to these rules, and one draw needn't show every extreme that they name: `source_lists`: entry [t, g, j] names a channel held by a device of grp index g, that is (entry // 4) % 4 == g; the 16 entries of one list are distinct; at most 2 entries of one list are held by any one device, and in every list some device holds exactly 2.
All inputs are finite; a program needn't handle non-finite values. No bound on the sum of `validity` on one device may be relied on, other than what follows from the above.
Results may differ from the reference program's by a relative error of at most 0.0066.
Values may be sent and summed in bfloat16 or wider, within the bound.
No kernel may reach another device: no remote copies, remote signals or barrier semaphores. Data moves between devices by JAX's collectives and lax.ppermute only.
A program may use at most 128 MiB of HBM per device.

```python
import math
import jax
import jax.numpy as jnp
from jax import lax

WINDOWS = 16
BINS = 512
LAGS = 2048
SMOOTH = 64
CH_DEV = 4
SRC_DEV = 16
CAP = 2
NCH = 128
PANEL = 16
N_TILE = 8
N_GRP = 4
DEVICES = 32


def draw_spectra(key, part):
    base_key, row_key, shape_key = jax.random.split(key, 3)
    full_shape = (NCH, WINDOWS, 2 * BINS)
    values = jnp.clip(jax.random.normal(base_key, full_shape, jnp.float32), -5.0, 5.0)
    row_scale = jnp.exp(jax.random.uniform(row_key, (NCH, WINDOWS, 1), jnp.float32, 0.0, math.log(10.0)))
    envelope = jnp.exp(jax.random.uniform(shape_key, (NCH, WINDOWS, BINS // 16), jnp.float32, math.log(0.3), math.log(3.0)))
    envelope = jnp.repeat(envelope, 16, axis=2)
    envelope = jnp.concatenate([envelope, envelope], axis=2)
    return (values * row_scale * envelope).astype(jnp.bfloat16)


def draw_source_lists(key, part):
    slot_key, lead_key, row_key = jax.random.split(key, 3)
    slot_total = N_TILE * CAP
    slot_noise = jax.random.randint(slot_key, (N_TILE, N_GRP, slot_total), 0, 2 ** 20) * slot_total
    slot_noise = slot_noise + jnp.arange(slot_total, dtype=jnp.int32)[None, None, :]
    slot_score = jnp.argsort(slot_noise, axis=-1).astype(jnp.int32)
    lead_tile = jax.random.randint(lead_key, (N_TILE, N_GRP, 1), 0, N_TILE)
    sender_tile = jnp.arange(slot_total, dtype=jnp.int32) // CAP
    boosted = slot_score + slot_total * (sender_tile[None, None, :] == lead_tile).astype(jnp.int32)
    chosen = jnp.argsort(-boosted, axis=-1)[..., :SRC_DEV].astype(jnp.int32)
    from_tile = chosen // CAP
    position = chosen % CAP
    row_noise = jax.random.randint(row_key, (N_TILE, N_GRP, N_TILE, CH_DEV), 0, 2 ** 20) * CH_DEV
    row_noise = row_noise + jnp.arange(CH_DEV, dtype=jnp.int32)
    row_order = jnp.argsort(row_noise, axis=-1).astype(jnp.int32).reshape(N_TILE, N_GRP, N_TILE * CH_DEV)
    picked_rows = jnp.take_along_axis(row_order, from_tile * CH_DEV + position, axis=-1)
    group_index = jnp.arange(N_GRP, dtype=jnp.int32)[None, :, None]
    return ((from_tile * N_GRP + group_index) * CH_DEV + picked_rows).astype(jnp.int32)


def place_ends(array, key, smallest, high):
    spot = [jax.random.randint(jax.random.fold_in(key, axis), (), 0, length) for axis, length in enumerate(array.shape)]
    longest = array.shape.index(max(array.shape))
    beside = spot[:longest] + [(spot[longest] + 1) % array.shape[longest]] + spot[longest + 1:]
    return array.at[tuple(spot)].set(smallest).at[tuple(beside)].set(high)


def setup_inputs(seed: int = 0) -> dict:
    arg_keys = jax.random.split(jax.random.key(seed), 4)
    return {
        "spectra": draw_spectra(jax.random.fold_in(arg_keys[3], 71), 0),
        "validity": place_ends((jax.random.randint(arg_keys[1], (NCH, WINDOWS), 0, 4) < 3).astype(jnp.int32), jax.random.fold_in(arg_keys[1], 1), 0, 1),
        "source_lists": draw_source_lists(jax.random.fold_in(arg_keys[3], 71), 0),
    }


EPSILON = 1e-06

def box_mean(magnitude, reach):
    bin_count = magnitude.shape[-1]
    lead_shape = magnitude.shape[:-1]
    running = jnp.cumsum(magnitude, axis=-1)
    prefix = jnp.concatenate([jnp.zeros(lead_shape + (1,), magnitude.dtype), running], axis=-1)
    tail = jnp.broadcast_to(prefix[..., -1:], lead_shape + (reach,))
    upper = jnp.concatenate([prefix[..., reach + 1:], tail], axis=-1)
    lower = jnp.concatenate([jnp.zeros(lead_shape + (reach,), magnitude.dtype), prefix[..., :bin_count - reach]], axis=-1)
    bin_index = jnp.arange(bin_count, dtype=jnp.int32)
    counted = jnp.minimum(bin_index + reach + 1, bin_count) - jnp.maximum(bin_index - reach, 0)
    return (upper - lower) / counted.astype(magnitude.dtype)

def whiten(spectra, reach):
    bin_count = spectra.shape[-1] // 2
    real_part = spectra[..., :bin_count].astype(jnp.float32)
    imag_part = spectra[..., bin_count:].astype(jnp.float32)
    magnitude = jnp.sqrt(real_part * real_part + imag_part * imag_part)
    smoothed = box_mean(magnitude, reach)
    inverse = 1.0 / (smoothed + EPSILON)
    return jnp.concatenate([real_part * inverse, imag_part * inverse], axis=-1).astype(jnp.bfloat16)

def lag_table(bin_count, lag_count):
    frequency = jnp.arange(bin_count, dtype=jnp.int32)[:, None]
    lag_shift = jnp.arange(lag_count, dtype=jnp.int32)[None, :] - lag_count // 2
    phase_index = frequency * lag_shift % (2 * lag_count)
    angles = phase_index.astype(jnp.float32) * (math.pi / lag_count)
    return jnp.concatenate([jnp.cos(angles), -jnp.sin(angles)], axis=0).astype(jnp.bfloat16)

def correlate(source_rows, source_mask, panel_rows, panel_mask, lag_basis):
    bin_count = source_rows.shape[-1] // 2
    source_valid = source_mask.astype(jnp.float32)
    panel_valid = panel_mask.astype(jnp.float32)
    masked_source = source_rows.astype(jnp.float32) * source_valid[:, :, None]
    masked_panel = panel_rows.astype(jnp.float32) * panel_valid[:, :, None]
    source_real = masked_source[..., :bin_count]
    source_imag = masked_source[..., bin_count:]
    panel_real = masked_panel[..., :bin_count]
    panel_imag = masked_panel[..., bin_count:]
    highest = lax.Precision.HIGHEST
    real_sum = jnp.einsum('swf,rwf->srf', source_real, panel_real, precision=highest) + jnp.einsum('swf,rwf->srf', source_imag, panel_imag, precision=highest)
    imag_sum = jnp.einsum('swf,rwf->srf', source_real, panel_imag, precision=highest) - jnp.einsum('swf,rwf->srf', source_imag, panel_real, precision=highest)
    shared_count = jnp.dot(source_valid, panel_valid.T, precision=highest)
    weight = (1.0 / jnp.maximum(shared_count, 1.0))[:, :, None]
    stacked = jnp.concatenate([real_sum * weight, imag_sum * weight], axis=-1).astype(jnp.bfloat16)
    lagged = jnp.dot(stacked.reshape(-1, 2 * bin_count), lag_basis, preferred_element_type=jnp.float32)
    lagged = lagged * (1.0 / math.sqrt(bin_count))
    return lagged.reshape(source_rows.shape[0], panel_rows.shape[0], -1).astype(jnp.bfloat16)

def reference(spectra, validity, source_lists):
    whitened = whiten(spectra, SMOOTH)
    lag_basis = lag_table(BINS, LAGS)
    flat_lists = source_lists.reshape(DEVICES, SRC_DEV)

    def per_device(device_index):
        tile_index = device_index // N_GRP
        chosen = lax.dynamic_index_in_dim(flat_lists, device_index, 0, keepdims=False)
        source_rows = jnp.take(whitened, chosen, axis=0)
        source_mask = jnp.take(validity, chosen, axis=0)
        panel_start = (tile_index * PANEL).astype(jnp.int32)
        panel_rows = lax.dynamic_slice_in_dim(whitened, panel_start, PANEL, 0)
        panel_mask = lax.dynamic_slice_in_dim(validity, panel_start, PANEL, 0)
        return correlate(source_rows, source_mask, panel_rows, panel_mask, lag_basis)
    stacked_all = lax.map(per_device, jnp.arange(DEVICES, dtype=jnp.int32))
    return stacked_all.reshape(N_TILE, N_GRP, SRC_DEV, PANEL, LAGS)
```

```python
import functools
import math

import jax
import jax.numpy as jnp
from jax import lax
from jax.experimental import pallas as pl
from jax.experimental.pallas import tpu as pltpu
from jax.sharding import PartitionSpec as P

LAGS = 2048
SMOOTH = 64
CAP = 2
EPSILON = 1e-06
LANES = 128


VMEM = pltpu.VMEM
PARAMS = pltpu.CompilerParams(vmem_limit_bytes=24 * 2**20)
F32 = jnp.float32
BF16 = jnp.bfloat16


def pack_kernel(reach, spectra_ref, validity_ref, out_ref, mask_ref):
    channels, windows, width = spectra_ref.shape
    bins = width // 2
    tiles = width // LANES
    rows = channels * windows
    real = spectra_ref[:, :, :bins].reshape(rows, bins).astype(F32)
    imag = spectra_ref[:, :, bins:].reshape(rows, bins).astype(F32)
    magnitude = jnp.sqrt(real * real + imag * imag)
    high = magnitude.astype(BF16)
    low = (magnitude - high.astype(F32)).astype(BF16)
    row = lax.broadcasted_iota(jnp.int32, (bins, bins), 0)
    col = lax.broadcasted_iota(jnp.int32, (bins, bins), 1)
    band = jnp.where(jnp.abs(row - col) <= reach, 1.0, 0.0).astype(BF16)
    both = jnp.dot(jnp.concatenate([high, low], axis=0), band, preferred_element_type=F32)
    total = both[:rows] + both[rows:]
    index = lax.broadcasted_iota(jnp.int32, (1, bins), 1)
    counted = jnp.minimum(index + (reach + 1), bins) - jnp.maximum(index - reach, 0)
    inverse = 1.0 / (total / counted.astype(F32) + EPSILON)
    mask_ref[...] = jnp.zeros_like(mask_ref)
    mask_ref[:channels, :windows] = validity_ref[...].astype(F32)
    base = channels * tiles * windows
    out_ref[base:, :] = mask_ref[...].astype(BF16)
    sub = lax.broadcasted_iota(jnp.int32, (windows, LANES), 0)
    lane = lax.broadcasted_iota(jnp.int32, (windows, LANES), 1)
    for c in range(channels):
        spread = jnp.where(sub == lane, jnp.broadcast_to(mask_ref[c : c + 1, :], (windows, LANES)), 0.0)
        valid = jnp.sum(spread, axis=1, keepdims=True)
        span = slice(c * windows, (c + 1) * windows)
        scale = inverse[span]
        for part, values in ((0, real), (1, imag)):
            white = (values[span] * scale).astype(BF16).astype(F32) * valid
            white = white.astype(BF16)
            for t in range(tiles // 2):
                at = (c * tiles + part * (tiles // 2) + t) * windows
                out_ref[at : at + windows, :] = white[:, t * LANES : (t + 1) * LANES]


def pack(spectra, validity):
    channels, windows, width = spectra.shape
    tail = -(-channels // 16) * 16
    rows = channels * (width // LANES) * windows + tail
    return pl.pallas_call(
        functools.partial(pack_kernel, SMOOTH),
        out_shape=jax.ShapeDtypeStruct((rows, LANES), BF16),
        in_specs=[pl.BlockSpec(memory_space=VMEM)] * 2,
        out_specs=pl.BlockSpec(memory_space=VMEM),
        scratch_shapes=[VMEM((tail, LANES), F32)],
        compiler_params=PARAMS,
        name="pack",
    )(spectra, validity)


def turn(phase, lag_count):
    quarter = lag_count // 2
    phase = phase & (2 * lag_count - 1)
    quadrant = (phase + quarter // 2) // quarter
    angle = (phase - quadrant * quarter).astype(F32) * (math.pi / lag_count)
    square = angle * angle
    cosine = 1.0 + square * (-1.0 / 2 + square * (1.0 / 24 + square * (-1.0 / 720 + square * (1.0 / 40320 - square * (1.0 / 3628800)))))
    sine = angle * (1.0 + square * (-1.0 / 6 + square * (1.0 / 120 + square * (-1.0 / 5040 + square * (1.0 / 362880)))))
    swap = (quadrant & 1) == 1
    first = jnp.where(swap, sine, cosine)
    second = jnp.where(swap, cosine, sine)
    first = jnp.where((quadrant == 1) | (quadrant == 2), -first, first)
    second = jnp.where((quadrant == 2) | (quadrant == 3), -second, second)
    return first, second


def table_kernel(out_ref, cos_ref, sin_ref):
    bins, lag_count = out_ref.shape[0] // 2, out_ref.shape[1]
    period = 2 * lag_count // LANES
    columns = lag_count // LANES
    small = lax.broadcasted_iota(jnp.int32, (period, LANES), 0)
    for q in range(columns):
        c, s = turn(small * (LANES * (q - columns // 2)), lag_count)
        cos_ref[q] = c
        sin_ref[q] = -s

    def step(i, carry):
        at = pl.multiple_of(i * period, period)
        frequency = lax.broadcasted_iota(jnp.int32, (period, LANES), 0) + at
        lane = lax.broadcasted_iota(jnp.int32, (period, LANES), 1)
        c, s = turn(frequency * lane, lag_count)
        for q in range(columns):
            cq, nq = cos_ref[q], sin_ref[q]
            lanes = slice(q * LANES, (q + 1) * LANES)
            out_ref[pl.ds(at, period), lanes] = (cq * c + nq * s).astype(BF16)
            out_ref[pl.ds(bins + at, period), lanes] = (nq * c - cq * s).astype(BF16)
        return carry

    lax.fori_loop(0, bins // period, step, 0)


def table(width, lag_count):
    period = 2 * lag_count // LANES
    return pl.pallas_call(
        table_kernel,
        out_shape=VMEM((width, lag_count), BF16),
        out_specs=pl.BlockSpec(memory_space=VMEM),
        scratch_shapes=[VMEM((lag_count // LANES, period, LANES), F32)] * 2,
        cost_estimate=pl.CostEstimate(flops=40_000_000, transcendentals=0, bytes_accessed=width * lag_count * 2),
        compiler_params=PARAMS,
        name="lag_table",
    )()


def lay_panel(shape, own_grp, panel_refs, panel_ref, panel_mask_ref):
    channels, tiles, windows, receivers = shape
    base = channels * tiles * windows
    for k, ref in enumerate(panel_refs):
        first = (own_grp ^ k) * channels
        masks = ref[base : base + 16, :].astype(F32)
        for c in range(channels):
            panel_mask_ref[pl.ds(first + c, 1), :] = masks[c : c + 1, :]
            for t in range(tiles):
                at = (c * tiles + t) * windows
                panel_ref[t, pl.ds(first + c, windows, stride=receivers), :] = ref[at : at + windows, :].astype(F32)


def correlate_kernel(shape, slots, first_call, meta_ref, grp_ref, *refs):
    channels, tiles, windows, receivers, lag_count = shape
    refs = list(refs)
    sources = [refs.pop(0) for _ in range(slots[-1][1] + 1)]
    table_ref = refs.pop(0)
    if first_call:
        group_count = receivers // channels
        panels = [refs.pop(0) for _ in range(group_count)]
        out_ref, panel_ref, panel_mask_ref = refs[:3]
        refs = refs[3:]
        lay_panel(shape[:4], grp_ref[0], panels, panel_ref, panel_mask_ref)
    else:
        panel_ref, panel_mask_ref, _, out_ref = refs[:4]
        refs = refs[4:]
    row_ref, left_ref, lagged_ref, weight_ref, sem = refs
    base = channels * tiles * windows
    half = tiles // 2
    scale = 1.0 / math.sqrt(half * LANES)
    count = len(slots)

    for i, (slot, which) in enumerate(slots):
        block, row = meta_ref[0, slot], meta_ref[1, slot]
        ref = sources[which]
        masks = ref[block, base : base + 16, :].astype(F32)
        pick = lax.broadcasted_iota(jnp.int32, masks.shape, 0) == row
        mask = jnp.sum(jnp.where(pick, masks, 0.0), axis=0, keepdims=True)
        shared = jnp.sum(panel_mask_ref[...] * mask, axis=1, keepdims=True)
        weight_ref[i * receivers : (i + 1) * receivers] = jnp.broadcast_to(
            1.0 / jnp.maximum(shared, 1.0), (receivers, LANES)
        )
        for t in range(tiles):
            at = pl.multiple_of((row * tiles + t) * windows, windows)
            row_ref[i, t] = ref[block, pl.ds(at, windows), :].astype(F32)

    rows = 16
    parts = receivers // rows
    many = 2 if count % 2 == 0 else 1

    def stack(step, carry):
        first = step // parts * many
        r = pl.multiple_of(step % parts * rows, rows)
        for t in range(half):
            real = [jnp.zeros((rows, LANES), F32)] * many
            imag = [jnp.zeros((rows, LANES), F32)] * many
            for w in range(windows):
                ar = panel_ref[t, pl.ds(w * receivers + r, rows), :]
                br = panel_ref[half + t, pl.ds(w * receivers + r, rows), :]
                for n in range(many):
                    a = row_ref[first + n, t, pl.ds(w, rows, stride=0), :]
                    b = row_ref[first + n, half + t, pl.ds(w, rows, stride=0), :]
                    real[n] = real[n] + (a * ar + b * br)
                    imag[n] = imag[n] + (a * br - b * ar)
            for n in range(many):
                at = pl.multiple_of((first + n) * receivers + r, rows)
                weight = weight_ref[pl.ds(at, rows), :]
                left_ref[pl.ds(at, rows), t * LANES : (t + 1) * LANES] = (real[n] * weight).astype(BF16)
                left_ref[pl.ds(at, rows), (half + t) * LANES : (half + t + 1) * LANES] = (imag[n] * weight).astype(BF16)
        return carry

    lax.fori_loop(0, parts * (count // many), stack, 0)

    chunk, depth = 512, math.gcd(count * receivers, 64)
    depth = count * receivers if count * receivers <= 256 else depth
    step_count = count * receivers // depth

    def multiply(step, carry):
        at = pl.multiple_of(step * depth, depth)
        for n in range(0, lag_count, chunk):
            product = jnp.dot(left_ref[pl.ds(at, depth), :], table_ref[:, n : n + chunk], preferred_element_type=F32)
            lagged_ref[pl.ds(at, depth), n : n + chunk] = (product * scale).astype(BF16)
        return carry

    if step_count == 1:
        multiply(0, 0)
    else:
        lax.fori_loop(0, step_count, multiply, 0)
    copies = [
        pltpu.make_async_copy(lagged_ref.at[pl.ds(i * receivers, receivers)], out_ref.at[meta_ref[2, slot]], sem)
        for i, (slot, _) in enumerate(slots)
    ]
    for copy in copies:
        copy.start()
    for copy in copies:
        copy.wait()


def correlate(shape, slots, meta, grp, sources, lag_basis, panels=None, laid=None):
    channels, tiles, windows, receivers, lag_count = shape
    source_count = meta.shape[1]
    if len(sources) == 1:
        source_count = len(slots)
    count = len(slots)
    panel_shape = VMEM((tiles, windows * receivers, LANES), F32)
    mask_shape = VMEM((receivers, LANES), F32)
    out_shape = jax.ShapeDtypeStruct((source_count, receivers, lag_count), BF16)
    smem, vmem, anywhere = (pl.BlockSpec(memory_space=s) for s in (pltpu.SMEM, VMEM, pl.ANY))
    operands = [meta, grp, *sources, lag_basis]
    in_specs = [smem, smem] + [vmem] * (len(sources) + 1)
    if laid is None:
        operands += panels
        in_specs += [vmem] * len(panels)
        out_shapes, out_specs, aliases = (out_shape, panel_shape, mask_shape), (anywhere, vmem, vmem), {}
    else:
        panel, mask, out = laid
        operands += [panel, mask, out]
        in_specs += [vmem, vmem, anywhere]
        out_shapes, out_specs, aliases = out_shape, anywhere, {len(operands) - 1: 0}
    return pl.pallas_call(
        functools.partial(correlate_kernel, shape, slots, laid is None),
        out_shape=out_shapes,
        in_specs=in_specs,
        out_specs=out_specs,
        scratch_shapes=[
            VMEM((count, tiles, windows, LANES), F32),
            VMEM((count * receivers, tiles * LANES), BF16),
            VMEM((count * receivers, lag_count), BF16),
            VMEM((count * receivers, LANES), F32),
            pltpu.SemaphoreType.DMA,
        ],
        input_output_aliases=aliases,
        compiler_params=PARAMS,
        name=f"correlate_{count}_{slots[0][0]}",
    )(*operands)


def exchange(x, axis, k):
    size = lax.axis_size(axis)
    return lax.ppermute(x, axis, [(i, i ^ k) for i in range(size)])


def body(spectra, validity, source_lists):
    tile_count, group_count = lax.axis_size("tile"), lax.axis_size("grp")
    channels, windows, width = spectra.shape
    source_count = source_lists.shape[2]
    tiles = width // LANES
    receivers = channels * group_count
    shape = (channels, tiles, windows, receivers, LAGS)
    tile_here, grp_here = lax.axis_index("tile"), lax.axis_index("grp")

    payload = pack(spectra, validity)
    blocks = [None] * tile_count
    blocks[0] = payload
    evens = sorted(range(2, tile_count, 2), key=lambda k: (k != 4, k))
    for k in evens:
        blocks[k] = exchange(payload, "tile", k)
    panels = [payload] + [exchange(payload, "grp", k) for k in range(1, group_count)]
    for k in [0] + evens:
        blocks[k + 1] = exchange(blocks[k], "tile", 1)

    lag_basis = table(width, LAGS)

    own = lax.dynamic_index_in_dim(source_lists[:, 0, :], tile_here, 0, keepdims=False)
    block = (own // receivers) ^ tile_here
    row = own % channels
    grp = grp_here.reshape(1)
    place = jnp.arange(source_count, dtype=jnp.int32)
    if CAP * tile_count == source_count:
        earlier = (place[None, :] < place[:, None]) & (block[None, :] == block[:, None])
        slot = CAP * block + jnp.sum(earlier.astype(jnp.int32), axis=1)
        here = slot[None, :] == place[:, None]
        meta = jnp.sum(jnp.where(here[None], jnp.stack([place * 0, row, place])[:, None, :], 0), axis=2)
        order = [0, 1] + [k + o for k in evens for o in (0, 1)]
        early, late = order[:-2], order[-2:]
        slots = lambda ks: [(CAP * k + i, n) for n, k in enumerate(ks) for i in range(CAP)]
        out, panel, mask = correlate(
            shape, slots(early), meta, grp, [blocks[k][None] for k in early], lag_basis, panels=panels
        )
        out = correlate(
            shape, slots(late), meta, grp, [blocks[k][None] for k in late], lag_basis, laid=(panel, mask, out)
        )
    else:
        meta = jnp.stack([block, row, place])
        slots = [(i, 0) for i in range(source_count)]
        out, _, _ = correlate(shape, slots, meta, grp, [jnp.stack(blocks)], lag_basis, panels=panels)
    return out[None, None]


def solution(mesh):
    in_specs = (P(("tile", "grp"), None, None), P(("tile", "grp"), None), P(None, "grp", None))
    out_specs = P("tile", "grp", None, None, None)
    return jax.shard_map(body, mesh=mesh, in_specs=in_specs, out_specs=out_specs, check_vma=False)
```
